32 devices in a mesh: sp: 8 (over y, x, core), tp: 4 (over z).
Axes of the slice: x: 2, y: 2, z: 4, core: 2. Of those that a mesh axis runs over, the one named last changes fastest.
Arguments:
- queries: bfloat16 [4096, 8192], P('sp', 'tp'), may hold values from -200 to 200
- keys: bfloat16 [4096, 1024], P('sp', 'tp'), may hold values from -6 to 6
- values: bfloat16 [4096, 1024], P('sp', 'tp'), may hold values from -6 to 6
- w_out: bfloat16 [8192, 4096], P('tp'), may hold values from -0.0625 to 0.0625
- lengths: int32 [1], replicated, may hold values from 1 to 4096
- stretch_owner: int32 [8], replicated, may hold values from 0 to 7, as said below
- home_replica: int32 [1], replicated, may hold values from 0 to 7, as said below
Outputs:
- mixed: bfloat16 [4096, 4096], P(('sp', 'tp'))
- cache_keys: bfloat16 [32768, 1024], P('sp', 'tp')
- home_cache_values: bfloat16 [32768, 1024], P('sp', 'tp')
The draws below stay inside these ranges and needn't reach their ends.
Inputs may be any that keep to these rules, and one draw needn't show every extreme that they name: Stretch c of prompt p stands on replica stretch_owner[p * 8 + c]; every replica appears once. `home_replica`: the prompts' home replicas are distinct; prompt 0's home is (stretch_owner[0] + 8 / 2) modulo 8.
All inputs are finite; a program needn't handle non-finite values.
Results may differ from the reference program's by a relative error of at most 0.014.
Values may be sent and summed in bfloat16 or wider, within the bound.
A program may use at most 128 MiB of HBM per device.

```python
import jax
import jax.numpy as jnp
from jax import lax

D = 4096
HEADS = 64
KV_HEADS = 8
HEAD_DIM = 128
STRETCH = 512
MAX_STRETCHES = 8
PROMPTS = 1
TOKENS = 4096
CACHE_ROWS = 32768
N_SP = 8
N_TP = 4


def pair_draw(key):
    base = jax.random.fold_in(key, 11)
    key_part, query_part = jax.random.split(base, 2)
    key_rows = jnp.clip(jax.random.normal(key_part, (TOKENS, KV_HEADS * HEAD_DIM), jnp.float32), -6.0, 6.0)
    query_rows = jnp.clip(jax.random.normal(query_part, (TOKENS, HEADS * HEAD_DIM), jnp.float32), -6.0, 6.0)
    return (query_rows, key_rows)


def draw_queries(key, part):
    return pair_draw(key)[0].astype(jnp.bfloat16)


def draw_keys(key, part):
    return pair_draw(key)[1].astype(jnp.bfloat16)


def placement_draw(key):
    owner_list = jax.random.permutation(jax.random.fold_in(key, 7), N_SP).astype(jnp.int32)
    first_home = (owner_list[0] + N_SP // 2) % N_SP
    shuffled = jax.random.permutation(jax.random.fold_in(key, 5), N_SP).astype(jnp.int32)
    order_index = jnp.argsort((shuffled == first_home).astype(jnp.int32), stable=True)
    remaining = shuffled[order_index]
    homes = jnp.concatenate([first_home[None], remaining[:PROMPTS - 1]], 0).astype(jnp.int32)
    return (owner_list, homes)


def draw_stretch_owner(key, part):
    return placement_draw(key)[0]


def draw_home_replica(key, part):
    return placement_draw(key)[1]


def steps_of(stream_key, extent, cuts, low, high):
    factor_of, own = 1.0, jax.random.fold_in(stream_key, 6)
    for position, parts in cuts:
        heights = jnp.exp(jax.random.uniform(jax.random.fold_in(own, position), (parts,), jnp.float32, low / len(cuts), high / len(cuts)))
        factor_of = factor_of * jnp.repeat(heights, extent[position] // parts).reshape([-1 if axis == position else 1 for axis in range(len(extent))])
    return factor_of


def gaussian(stream_key, shape, width, bound, cuts=(), kind=jnp.bfloat16):
    level = steps_of(stream_key, shape, cuts, -0.22, 0.18) if cuts else 1.0
    drawn = jax.random.normal(stream_key, shape, jnp.float32) * width * level
    return jnp.minimum(jnp.maximum(drawn, -bound), bound).astype(kind)


def setup_inputs(seed: int = 0) -> dict:
    arg_keys = jax.random.split(jax.random.key(seed), 8)
    queries = draw_queries(jax.random.fold_in(arg_keys[7], 71), 0)
    keys = draw_keys(jax.random.fold_in(arg_keys[7], 71), 0)
    values = gaussian(arg_keys[2], (TOKENS, KV_HEADS * HEAD_DIM), 1.0, 6.0, ((0, 8), (1, 4)))
    w_out = gaussian(arg_keys[3], (HEADS * HEAD_DIM, D), (HEADS * HEAD_DIM) ** -0.5, 0.0625, ((0, 4),))
    lengths = jax.random.randint(arg_keys[4], (PROMPTS,), 1, MAX_STRETCHES * STRETCH + 1).astype(jnp.int32)
    stretch_owner = draw_stretch_owner(jax.random.fold_in(arg_keys[7], 71), 0)
    home_replica = draw_home_replica(jax.random.fold_in(arg_keys[7], 71), 0)
    return {"queries": queries, "keys": keys, "values": values, "w_out": w_out, "lengths": lengths, "stretch_owner": stretch_owner, "home_replica": home_replica}


def reference(queries, keys, values, w_out, lengths, stretch_owner, home_replica):
    group_size = HEADS // KV_HEADS
    score_scale = HEAD_DIM ** -0.5
    cache_span = MAX_STRETCHES * STRETCH
    positions = jnp.arange(cache_span, dtype=jnp.int32)
    attended = jnp.zeros((TOKENS, HEADS * HEAD_DIM), jnp.bfloat16)
    cache_keys = jnp.zeros((CACHE_ROWS, KV_HEADS * HEAD_DIM), jnp.bfloat16)
    home_cache_values = jnp.zeros((CACHE_ROWS, KV_HEADS * HEAD_DIM), jnp.bfloat16)
    for prompt in range(PROMPTS):
        slot_ids = stretch_owner[prompt * MAX_STRETCHES:(prompt + 1) * MAX_STRETCHES].astype(jnp.int32)
        row_ids = (slot_ids[:, None] * STRETCH + jnp.arange(STRETCH, dtype=jnp.int32)[None, :]).reshape(-1)
        prompt_queries = queries[row_ids]
        prompt_keys = keys[row_ids]
        prompt_values = values[row_ids]
        live_rows = positions < lengths[prompt]
        visible = (positions[None, :] <= positions[:, None]) & live_rows[None, :]
        query_head_rows = prompt_queries.astype(jnp.float32).reshape(cache_span, HEADS, HEAD_DIM).transpose(1, 0, 2)
        key_heads = prompt_keys.astype(jnp.float32).reshape(cache_span, KV_HEADS, HEAD_DIM).transpose(1, 0, 2)
        value_heads = prompt_values.astype(jnp.float32).reshape(cache_span, KV_HEADS, HEAD_DIM).transpose(1, 0, 2)
        key_heads = jnp.repeat(key_heads, group_size, axis=0)
        value_heads = jnp.repeat(value_heads, group_size, axis=0)

        def one_head(operands):
            query_one, key_one, value_one = operands
            scores = jnp.einsum("id,jd->ij", query_one, key_one) * score_scale
            scores = jnp.where(visible, scores, -1e30)
            largest = jnp.max(scores, axis=-1, keepdims=True)
            weights = jnp.where(visible, jnp.exp(scores - largest), 0.0)
            totals = jnp.sum(weights, axis=-1, keepdims=True)
            rounded = lax.optimization_barrier(weights.astype(jnp.bfloat16)).astype(jnp.float32)
            return jnp.einsum("ij,jd->id", rounded, value_one) / totals

        outputs = lax.map(one_head, (query_head_rows, key_heads, value_heads))
        outputs = outputs.transpose(1, 0, 2).reshape(cache_span, HEADS * HEAD_DIM)
        outputs = outputs * live_rows[:, None].astype(jnp.float32)
        attended = attended.at[row_ids].set(outputs.astype(jnp.bfloat16))
        kept_keys = jnp.where(live_rows[:, None], prompt_keys, jnp.zeros_like(prompt_keys))
        kept_values = jnp.where(live_rows[:, None], prompt_values, jnp.zeros_like(prompt_values))
        start_row = (home_replica[prompt] * cache_span).astype(jnp.int32)
        zero_column = jnp.zeros((), jnp.int32)
        cache_keys = lax.dynamic_update_slice(cache_keys, kept_keys, (start_row, zero_column))
        home_cache_values = lax.dynamic_update_slice(home_cache_values, kept_values, (start_row, zero_column))
    group_cols = HEADS * HEAD_DIM // N_TP
    mixed_sum = jnp.zeros((TOKENS, D), jnp.float32)
    for group in range(N_TP):
        partial_value = jnp.dot(attended[:, group * group_cols:(group + 1) * group_cols], w_out[group * group_cols:(group + 1) * group_cols], preferred_element_type=jnp.float32)
        partial_value = lax.optimization_barrier(partial_value.astype(jnp.bfloat16)).astype(jnp.float32)
        mixed_sum = mixed_sum + partial_value
    mixed = mixed_sum.astype(jnp.bfloat16)
    return (mixed, cache_keys, home_cache_values)
```

```python
import functools
import math

import jax
import jax.numpy as jnp
from jax import lax
from jax.experimental import pallas as pl
from jax.experimental.pallas import tpu as pltpu
from jax.sharding import PartitionSpec as P

HEAD_DIM = 128
MAX_STRETCHES = 8
CHUNKS = 2
UNROLL = 4
LOG2E = math.log2(math.e)
FAR = -1e30


def find(table, value):
    index = jnp.int32(0)
    for j in range(table.shape[0]):
        index = index + jnp.where(table[j] == value, j, 0)
    return index


def attend_kernel(
    chunk, stretch, heads, place, owner_ref, length_ref, home_ref, q_ref, k_ref, v_ref, o_ref, *rest
):
    me = lax.axis_index("sp")
    mine = find(owner_ref, me)
    prompt = mine // MAX_STRETCHES
    own = mine % MAX_STRETCHES
    length = length_ref[prompt]
    parts, _, rows, _ = q_ref.shape
    lanes = parts * rows
    span = MAX_STRETCHES * stretch

    if place:
        kc_ref, vc_ref, stage, sems = rest
        group, turn = pl.program_id(0), pl.program_id(1)
        columns = pl.ds(pl.multiple_of(group * HEAD_DIM, HEAD_DIM), HEAD_DIM)
        copies = [
            pltpu.make_async_copy(stage.at[i], out.at[:, columns], sems.at[i])
            for i, out in enumerate((kc_ref, vc_ref))
        ]

        @pl.when(turn == 0)
        def _():
            homed = jnp.int32(0)
            kept = jnp.int32(0)
            for p in range(home_ref.shape[0]):
                here = home_ref[p] == me
                homed = jnp.where(here, p, homed)
                kept = jnp.where(here, length_ref[p], kept)

            def fill(j, _):
                start = pl.multiple_of(owner_ref[homed * MAX_STRETCHES + j] * stretch, stretch)
                target = pl.ds(pl.multiple_of(j * stretch, stretch), stretch)
                position = j * stretch + lax.broadcasted_iota(jnp.int32, (stretch, HEAD_DIM), 0)
                for i, source in enumerate((k_ref, v_ref)):
                    block = source[pl.ds(start, stretch), :]
                    stage[i, target, :] = jnp.where(position < kept, block, jnp.zeros_like(block))
                return 0

            lax.fori_loop(0, MAX_STRETCHES, fill, 0)
            for copy in copies:
                copy.start()

    lane = lax.broadcasted_iota(jnp.int32, (1, lanes), 1)
    within = lane // rows * (stretch // parts) + chunk * rows + lane % rows
    live = own * stretch < length

    @pl.when(live)
    def _():
        scale = HEAD_DIM ** (-0.5) * LOG2E

        def step(j, state, masked):
            start = pl.multiple_of(owner_ref[prompt * MAX_STRETCHES + j] * stretch, stretch)
            key = k_ref[pl.ds(start, stretch), :]
            value = v_ref[pl.ds(start, stretch), :]
            fresh = []
            for u in range(heads):
                top, total, acc = state[u]
                query = q_ref[:, 0, :, u * HEAD_DIM : (u + 1) * HEAD_DIM].reshape(lanes, HEAD_DIM)
                scores = (
                    lax.dot_general(
                        key, query, (((1,), (1,)), ((), ())), preferred_element_type=jnp.float32
                    )
                    * scale
                )
                if masked:
                    place_of = lax.broadcasted_iota(jnp.int32, (stretch, lanes), 0)
                    scores = jnp.where(place_of <= within, scores, FAR)
                new_top = jnp.maximum(top, jnp.max(scores, axis=0, keepdims=True))
                weights = jnp.exp2(scores - new_top)
                rescale = jnp.exp2(top - new_top)
                total = total * rescale + jnp.sum(weights, axis=0, keepdims=True)
                acc = acc * rescale + lax.dot_general(
                    value,
                    weights.astype(jnp.bfloat16),
                    (((0,), (0,)), ((), ())),
                    preferred_element_type=jnp.float32,
                )
                fresh.append((new_top, total, acc))
            return tuple(fresh)

        empty = (
            jnp.full((1, lanes), FAR, jnp.float32),
            jnp.zeros((1, lanes), jnp.float32),
            jnp.zeros((HEAD_DIM, lanes), jnp.float32),
        )
        state = lax.fori_loop(
            0, own, functools.partial(step, masked=False), tuple(empty for _ in range(heads))
        )
        state = step(own, state, True)
        alive = (own * stretch + within < length).astype(jnp.float32)
        for u in range(heads):
            top, total, acc = state[u]
            out = (acc * (alive / total)).T
            o_ref[:, u * HEAD_DIM : (u + 1) * HEAD_DIM] = out.astype(jnp.bfloat16)

    @pl.when(jnp.logical_not(live))
    def _():
        o_ref[...] = jnp.zeros_like(o_ref)

    if place:

        @pl.when(turn == pl.num_programs(1) - 1)
        def _():
            for copy in copies:
                copy.wait()


def attend(chunk, place, stretch, tables, queries, keys, values):
    parts, _, rows, width = queries.shape
    kv_width = keys.shape[1]
    local_kv = kv_width // HEAD_DIM
    group_size = width // kv_width
    heads = math.gcd(UNROLL, group_size)
    turns = group_size // heads
    lanes = parts * rows
    span = MAX_STRETCHES * stretch
    out_shape = [jax.ShapeDtypeStruct((lanes, width), jnp.bfloat16)]
    out_specs = [pl.BlockSpec((lanes, heads * HEAD_DIM), lambda g, u, *_: (0, g * turns + u))]
    scratch = []
    if place:
        out_shape += [jax.ShapeDtypeStruct((span, kv_width), jnp.bfloat16)] * 2
        out_specs += [pl.BlockSpec(memory_space=pl.ANY)] * 2
        scratch = [
            pltpu.VMEM((2, span, HEAD_DIM), jnp.bfloat16),
            pltpu.SemaphoreType.DMA((2,)),
        ]
    pairs = lanes * span // 2 * (width // HEAD_DIM)
    return pl.pallas_call(
        functools.partial(attend_kernel, chunk, stretch, heads, place),
        out_shape=out_shape,
        grid_spec=pltpu.PrefetchScalarGridSpec(
            num_scalar_prefetch=3,
            grid=(local_kv, turns),
            in_specs=[
                pl.BlockSpec(
                    (parts, 1, rows, heads * HEAD_DIM), lambda g, u, *_: (0, chunk, 0, g * turns + u)
                ),
                pl.BlockSpec((keys.shape[0], HEAD_DIM), lambda g, u, *_: (0, g)),
                pl.BlockSpec((keys.shape[0], HEAD_DIM), lambda g, u, *_: (0, g)),
            ],
            out_specs=out_specs,
            scratch_shapes=scratch,
        ),
        compiler_params=pltpu.CompilerParams(
            dimension_semantics=("arbitrary", "arbitrary"), vmem_limit_bytes=48 * 2**20
        ),
        cost_estimate=pl.CostEstimate(
            flops=4 * pairs * HEAD_DIM, bytes_accessed=8 * lanes * width, transcendentals=pairs
        ),
        name=f"attend{chunk}",
    )(*tables, queries, keys, values)


def shards(queries, keys, values, w_out, lengths, stretch_owner, home_replica):
    stretch = queries.shape[0]
    parts = lax.axis_size("tp")
    rows = stretch // parts // CHUNKS
    tables = (stretch_owner, lengths, home_replica)
    split = queries.reshape(parts, CHUNKS, rows, queries.shape[1])
    all_keys = lax.all_gather(keys, "sp", axis=0, tiled=True)
    all_values = lax.all_gather(values, "sp", axis=0, tiled=True)
    pieces = []
    for chunk in range(CHUNKS):
        place = chunk == 0
        results = attend(chunk, place, stretch, tables, split, all_keys, all_values)
        if place:
            caches = results[1:]
        partial = jnp.dot(results[0], w_out, preferred_element_type=jnp.float32)
        pieces.append(
            lax.psum_scatter(partial.astype(jnp.bfloat16), "tp", scatter_dimension=0, tiled=True)
        )
    return (jnp.concatenate(pieces, axis=0), caches[0], caches[1])


def solution(mesh):
    placed = (P("sp", "tp"), P("sp", "tp"), P("sp", "tp"), P("tp", None), P(), P(), P())
    return jax.shard_map(
        shards,
        mesh=mesh,
        in_specs=placed,
        out_specs=(P(("sp", "tp"), None), P("sp", "tp"), P("sp", "tp")),
        check_vma=False,
    )
```

```python
import functools
import math

import jax
import jax.numpy as jnp
from jax import lax
from jax.experimental import pallas as pl
from jax.experimental.pallas import tpu as pltpu
from jax.sharding import PartitionSpec as P

HEAD_DIM = 128
MAX_STRETCHES = 8
ROW_BLOCK = 256
UNROLL = 4
LOG2E = math.log2(math.e)
FAR = -1e30
MESH = pl.DeviceIdType.MESH


def find(table, value):
    index = jnp.int32(0)
    for j in range(table.shape[0]):
        index = index + jnp.where(table[j] == value, j, 0)
    return index


def attend_kernel(
    stretch, heads, owner_ref, length_ref, home_ref, q_ref, k_ref, v_ref, o_ref, kc_ref, vc_ref,
    stage, sems,
):
    me = lax.axis_index("sp")
    mine = find(owner_ref, me)
    prompt = mine // MAX_STRETCHES
    own = mine % MAX_STRETCHES
    length = length_ref[prompt]
    lanes = q_ref.shape[0]
    group, block, turn = pl.program_id(0), pl.program_id(1), pl.program_id(2)
    columns = pl.ds(pl.multiple_of(group * HEAD_DIM, HEAD_DIM), HEAD_DIM)
    copies = [
        pltpu.make_async_copy(stage.at[i], out.at[:, columns], sems.at[i])
        for i, out in enumerate((kc_ref, vc_ref))
    ]

    @pl.when((block == 0) & (turn == 0))
    def _():
        homed = jnp.int32(0)
        kept = jnp.int32(0)
        for p in range(home_ref.shape[0]):
            here = home_ref[p] == me
            homed = jnp.where(here, p, homed)
            kept = jnp.where(here, length_ref[p], kept)

        def fill(j, _):
            start = pl.multiple_of(owner_ref[homed * MAX_STRETCHES + j] * stretch, stretch)
            target = pl.ds(pl.multiple_of(j * stretch, stretch), stretch)
            position = j * stretch + lax.broadcasted_iota(jnp.int32, (stretch, HEAD_DIM), 0)
            for i, source in enumerate((k_ref, v_ref)):
                block = source[pl.ds(start, stretch), :]
                stage[i, target, :] = jnp.where(position < kept, block, jnp.zeros_like(block))
            return 0

        lax.fori_loop(0, MAX_STRETCHES, fill, 0)
        for copy in copies:
            copy.start()

    within = block * lanes + lax.broadcasted_iota(jnp.int32, (1, lanes), 1)
    live = own * stretch + block * lanes < length

    @pl.when(live)
    def _():
        scale = HEAD_DIM ** (-0.5) * LOG2E

        def step(j, state, masked):
            start = pl.multiple_of(owner_ref[prompt * MAX_STRETCHES + j] * stretch, stretch)
            key = k_ref[pl.ds(start, stretch), :]
            value = v_ref[pl.ds(start, stretch), :]
            fresh = []
            for u in range(heads):
                top, total, acc = state[u]
                query = q_ref[:, u * HEAD_DIM : (u + 1) * HEAD_DIM]
                scores = (
                    lax.dot_general(
                        key, query, (((1,), (1,)), ((), ())), preferred_element_type=jnp.float32
                    )
                    * scale
                )
                if masked:
                    place_of = lax.broadcasted_iota(jnp.int32, (stretch, lanes), 0)
                    scores = jnp.where(place_of <= within, scores, FAR)
                new_top = jnp.maximum(top, jnp.max(scores, axis=0, keepdims=True))
                weights = jnp.exp2(scores - new_top)
                rescale = jnp.exp2(top - new_top)
                total = total * rescale + jnp.sum(weights, axis=0, keepdims=True)
                acc = acc * rescale + lax.dot_general(
                    value,
                    weights.astype(jnp.bfloat16),
                    (((0,), (0,)), ((), ())),
                    preferred_element_type=jnp.float32,
                )
                fresh.append((new_top, total, acc))
            return tuple(fresh)

        empty = (
            jnp.full((1, lanes), FAR, jnp.float32),
            jnp.zeros((1, lanes), jnp.float32),
            jnp.zeros((HEAD_DIM, lanes), jnp.float32),
        )
        state = lax.fori_loop(
            0, own, functools.partial(step, masked=False), tuple(empty for _ in range(heads))
        )
        state = step(own, state, True)
        alive = (own * stretch + within < length).astype(jnp.float32)
        for u in range(heads):
            top, total, acc = state[u]
            out = (acc * (alive / total)).T
            o_ref[:, u * HEAD_DIM : (u + 1) * HEAD_DIM] = out.astype(jnp.bfloat16)

    @pl.when(jnp.logical_not(live))
    def _():
        o_ref[...] = jnp.zeros_like(o_ref)

    @pl.when((block == pl.num_programs(1) - 1) & (turn == pl.num_programs(2) - 1))
    def _():
        for copy in copies:
            copy.wait()


def attend(stretch, tables, queries, keys, values):
    width = queries.shape[1]
    kv_width = keys.shape[1]
    local_kv = kv_width // HEAD_DIM
    group_size = width // kv_width
    heads = math.gcd(UNROLL, group_size)
    turns = group_size // heads
    lanes = math.gcd(ROW_BLOCK, stretch)
    span = MAX_STRETCHES * stretch
    cache = jax.ShapeDtypeStruct((span, kv_width), jnp.bfloat16)
    query_spec = pl.BlockSpec((lanes, heads * HEAD_DIM), lambda g, r, u, *_: (r, g * turns + u))
    kv_spec = pl.BlockSpec((keys.shape[0], HEAD_DIM), lambda g, r, u, *_: (0, g))
    return pl.pallas_call(
        functools.partial(attend_kernel, stretch, heads),
        out_shape=[jax.ShapeDtypeStruct((stretch, width), jnp.bfloat16), cache, cache],
        grid_spec=pltpu.PrefetchScalarGridSpec(
            num_scalar_prefetch=3,
            grid=(local_kv, stretch // lanes, turns),
            in_specs=[query_spec, kv_spec, kv_spec],
            out_specs=[query_spec] + [pl.BlockSpec(memory_space=pl.ANY)] * 2,
            scratch_shapes=[
                pltpu.VMEM((2, span, HEAD_DIM), jnp.bfloat16),
                pltpu.SemaphoreType.DMA((2,)),
            ],
        ),
        compiler_params=pltpu.CompilerParams(
            dimension_semantics=("arbitrary",) * 3, vmem_limit_bytes=48 * 2**20
        ),
        name="attend",
    )(*tables, queries, keys, values)


def gather_kernel(k_ref, v_ref, all_k, all_v, place_sem, send_sem, recv_sem):
    me = lax.axis_index("sp")
    rows = k_ref.shape[0]
    y, x, core = me // 4, me // 2 % 2, me % 2
    index = lambda y, x, core: y * 4 + x * 2 + core
    beside = index(y, 1 - x, core)
    above = index(1 - y, x, core)
    across = index(1 - y, 1 - x, core)
    partner = index(y, x, 1 - core)
    relay_from = core * beside + (1 - core) * above
    relay_to = core * above + (1 - core) * beside
    sources, outs = (k_ref, v_ref), (all_k, all_v)

    barrier = pltpu.get_barrier_semaphore()
    for other in (beside, above, partner):
        pl.semaphore_signal(barrier, inc=1, device_id={"sp": other}, device_id_type=MESH)
    pl.semaphore_wait(barrier, 3)

    def part(ref, owner):
        return ref.at[pl.ds(pl.multiple_of(owner * rows, rows), rows), :]

    def send(i, lane, source, owner, target):
        return pltpu.make_async_remote_copy(
            src_ref=source,
            dst_ref=part(outs[i], owner),
            send_sem=send_sem.at[lane, i],
            recv_sem=recv_sem.at[lane, i],
            device_id={"sp": target},
            device_id_type=MESH,
        )

    sent = []
    for i in range(2):
        for lane, target in ((0, beside), (1, above), (2, partner)):
            copy = send(i, lane, sources[i], me, target)
            copy.start()
            sent.append(copy)
        own = pltpu.make_async_copy(sources[i], part(outs[i], me), place_sem.at[i])
        own.start()
    relays = []
    for i in range(2):
        sent[3 * i].wait_recv()
        sent[3 * i + 1].wait_recv()
        relay = send(i, 3, part(outs[i], relay_from), relay_from, relay_to)
        relay.start()
        relays.append(relay)
        for lane, owner in ((4, beside), (5, above)):
            copy = send(i, lane, part(outs[i], owner), owner, partner)
            copy.start()
            relays.append(copy)
    last = []
    for i in range(2):
        relays[3 * i].wait_recv()
        copy = send(i, 6, part(outs[i], across), across, partner)
        copy.start()
        last.append(copy)
    for i in range(2):
        sent[3 * i + 2].wait_recv()
        relays[3 * i + 1].wait_recv()
        relays[3 * i + 2].wait_recv()
        last[i].wait_recv()
        pltpu.make_async_copy(sources[i], part(outs[i], me), place_sem.at[i]).wait()
    for copy in sent + relays + last:
        copy.wait_send()


def gather(keys, values):
    replicas = lax.axis_size("sp")
    if replicas != 8:
        return (
            lax.all_gather(keys, "sp", axis=0, tiled=True),
            lax.all_gather(values, "sp", axis=0, tiled=True),
        )
    shape = jax.ShapeDtypeStruct((replicas * keys.shape[0], keys.shape[1]), keys.dtype)
    return pl.pallas_call(
        gather_kernel,
        out_shape=[shape] * 2,
        in_specs=[pl.BlockSpec(memory_space=pltpu.VMEM)] * 2,
        out_specs=[pl.BlockSpec(memory_space=pl.ANY)] * 2,
        scratch_shapes=[
            pltpu.SemaphoreType.DMA((2,)),
            pltpu.SemaphoreType.DMA((7, 2)),
            pltpu.SemaphoreType.DMA((7, 2)),
        ],
        compiler_params=pltpu.CompilerParams(collective_id=0, has_side_effects=True),
        name="gather",
    )(keys, values)


def project_kernel(
    steps, a_ref, w_ref, o_ref, work, own, out_far, out_near, out_sum,
    in_far, in_near, in_sum, send_sem, recv_sem,
):
    me = lax.axis_index("tp")
    n = 4
    rows = a_ref.shape[0] // n
    step = pl.program_id(0)

    def hops(j):
        turn = 1 - 2 * (j % 2)
        return (me + turn + n) % n, (me - turn + n) % n

    def send(kind, j, target):
        source, dest = ((out_far, in_far), (out_near, in_near), (out_sum, in_sum))[kind]
        return pltpu.make_async_remote_copy(
            src_ref=source.at[j],
            dst_ref=dest.at[j],
            send_sem=send_sem.at[kind, j],
            recv_sem=recv_sem.at[kind, j],
            device_id={"tp": target},
            device_id_type=MESH,
        )

    @pl.when(step == 0)
    def _():
        barrier = pltpu.get_barrier_semaphore()
        for other in ((me + 1) % n, (me + n - 1) % n):
            pl.semaphore_signal(barrier, inc=1, device_id={"tp": other}, device_id_type=MESH)
        pl.semaphore_wait(barrier, 2)

    def rows_of(device):
        return pl.ds(pl.multiple_of(device * rows, rows), rows)

    def relay(j):
        toward, away = hops(j)
        send(0, j, toward).wait_recv()
        total = work[j % 2, rows_of(toward), :] + in_far[j].astype(jnp.float32)
        out_sum[j] = total.astype(jnp.bfloat16)
        send(2, j, toward).start()

    toward, away = hops(step)
    work[step % 2] = jnp.dot(a_ref[...], w_ref[...], preferred_element_type=jnp.float32)
    out_far[step] = work[step % 2, rows_of((me + 2) % n), :].astype(jnp.bfloat16)
    send(0, step, toward).start()
    out_near[step] = work[step % 2, rows_of(away), :].astype(jnp.bfloat16)
    send(1, step, away).start()
    own[step] = work[step % 2, rows_of(me), :]

    @pl.when(step > 0)
    def _():
        relay(step - 1)

    @pl.when(step == steps - 1)
    def _():
        relay(step)
        width = o_ref.shape[1] // steps
        for j in range(steps):
            toward, away = hops(j)
            send(1, j, away).wait_recv()
            send(2, j, toward).wait_recv()
            total = own[j] + in_near[j].astype(jnp.float32) + in_sum[j].astype(jnp.float32)
            o_ref[:, j * width : (j + 1) * width] = total.astype(jnp.bfloat16)
        for j in range(steps):
            toward, away = hops(j)
            send(0, j, toward).wait_send()
            send(1, j, away).wait_send()
            send(2, j, toward).wait_send()


def project(attended, w_out):
    if lax.axis_size("tp") != 4:
        partial = jnp.dot(attended, w_out, preferred_element_type=jnp.float32)
        return lax.psum_scatter(
            partial.astype(jnp.bfloat16), "tp", scatter_dimension=0, tiled=True
        )
    tokens, depth = attended.shape
    features = w_out.shape[1]
    rows = tokens // 4
    steps = 8
    width = features // steps
    buffer = pltpu.VMEM((steps, rows, width), jnp.bfloat16)
    return pl.pallas_call(
        functools.partial(project_kernel, steps),
        out_shape=jax.ShapeDtypeStruct((rows, features), jnp.bfloat16),
        grid=(steps,),
        in_specs=[
            pl.BlockSpec((tokens, depth), lambda j: (0, 0)),
            pl.BlockSpec((depth, width), lambda j: (0, j)),
        ],
        out_specs=pl.BlockSpec((rows, features), lambda j: (0, 0)),
        scratch_shapes=[
            pltpu.VMEM((2, tokens, width), jnp.float32),
            pltpu.VMEM((steps, rows, width), jnp.float32),
            buffer, buffer, buffer, buffer, buffer, buffer,
            pltpu.SemaphoreType.DMA((3, steps)),
            pltpu.SemaphoreType.DMA((3, steps)),
        ],
        compiler_params=pltpu.CompilerParams(
            collective_id=1,
            has_side_effects=True,
            dimension_semantics=("arbitrary",),
            vmem_limit_bytes=48 * 2**20,
        ),
        name="project",
    )(attended, w_out)


def shards(queries, keys, values, w_out, lengths, stretch_owner, home_replica):
    stretch = queries.shape[0]
    tables = (stretch_owner, lengths, home_replica)
    all_keys, all_values = gather(keys, values)
    attended, kept_keys, kept_values = attend(stretch, tables, queries, all_keys, all_values)
    return (project(attended, w_out), kept_keys, kept_values)


def solution(mesh):
    placed = (P("sp", "tp"), P("sp", "tp"), P("sp", "tp"), P("tp", None), P(), P(), P())
    return jax.shard_map(
        shards,
        mesh=mesh,
        in_specs=placed,
        out_specs=(P(("sp", "tp"), None), P("sp", "tp"), P("sp", "tp")),
        check_vma=False,
    )
```

```python
import functools
import math

import jax
import jax.numpy as jnp
from jax import lax
from jax.experimental import pallas as pl
from jax.experimental.pallas import tpu as pltpu
from jax.sharding import PartitionSpec as P

HEAD_DIM = 128
MAX_STRETCHES = 8
ROW_BLOCK = 512
UNROLL = 2
LOG2E = math.log2(math.e)
FAR = -1e30
MESH = pl.DeviceIdType.MESH


def find(table, value):
    index = jnp.int32(0)
    for j in range(table.shape[0]):
        index = index + jnp.where(table[j] == value, j, 0)
    return index


def attend_kernel(
    stretch, heads, owner_ref, length_ref, home_ref, q_ref, k_ref, v_ref, o_ref, kc_ref, vc_ref,
    stage, sems, top_ref, total_ref, acc_ref, vt_ref,
):
    me = lax.axis_index("sp")
    mine = find(owner_ref, me)
    prompt = mine // MAX_STRETCHES
    own = mine % MAX_STRETCHES
    length = length_ref[prompt]
    lanes = q_ref.shape[0]
    group, block, turn = pl.program_id(0), pl.program_id(1), pl.program_id(2)
    columns = pl.ds(pl.multiple_of(group * HEAD_DIM, HEAD_DIM), HEAD_DIM)
    copies = [
        pltpu.make_async_copy(stage.at[i], out.at[:, columns], sems.at[i])
        for i, out in enumerate((kc_ref, vc_ref))
    ]

    @pl.when((block == 0) & (turn == 0))
    def _():
        homed = jnp.int32(0)
        kept = jnp.int32(0)
        for p in range(home_ref.shape[0]):
            here = home_ref[p] == me
            homed = jnp.where(here, p, homed)
            kept = jnp.where(here, length_ref[p], kept)

        def fill(j, _):
            start = pl.multiple_of(owner_ref[homed * MAX_STRETCHES + j] * stretch, stretch)
            target = pl.ds(pl.multiple_of(j * stretch, stretch), stretch)
            position = j * stretch + lax.broadcasted_iota(jnp.int32, (stretch, HEAD_DIM), 0)
            for i, source in enumerate((k_ref, v_ref)):
                block = source[pl.ds(start, stretch), :]
                stage[i, target, :] = jnp.where(position < kept, block, jnp.zeros_like(block))
            return 0

        lax.fori_loop(0, MAX_STRETCHES, fill, 0)
        for copy in copies:
            copy.start()

        def turned(j, _):
            rows = pl.ds(pl.multiple_of(j * stretch, stretch), stretch)
            vt_ref[:HEAD_DIM, rows] = v_ref[rows, :].T
            return 0

        lax.fori_loop(0, v_ref.shape[0] // stretch, turned, 0)
        vt_ref[HEAD_DIM:, :] = jnp.ones((16, v_ref.shape[0]), jnp.bfloat16)

    within = block * lanes + lax.broadcasted_iota(jnp.int32, (1, lanes), 1)
    live = own * stretch + block * lanes < length

    @pl.when(live)
    def _():
        scale = HEAD_DIM ** (-0.5) * LOG2E

        def update(u, key, value, shown, top, total, acc):
            query = q_ref[:, u * HEAD_DIM : (u + 1) * HEAD_DIM]
            scores = lax.dot_general(
                key, query, (((1,), (1,)), ((), ())), preferred_element_type=jnp.float32
            )
            if shown is not None:
                scores = jnp.where(shown, scores, FAR)
            new_top = jnp.maximum(top, jnp.max(scores, axis=0, keepdims=True) * scale)
            weights = jnp.exp2(scores * scale - new_top)
            rescale = jnp.exp2(top - new_top)
            acc = acc * rescale + lax.dot_general(
                value, weights.astype(jnp.bfloat16), (((1,), (0,)), ((), ())),
                preferred_element_type=jnp.float32,
            )
            return new_top, total, acc

        def pieces(j, masked):
            start = pl.multiple_of(owner_ref[prompt * MAX_STRETCHES + j] * stretch, stretch)
            for first in range(0, stretch, 512):
                rows = pl.ds(start + first, 512)
                shown = None
                if masked:
                    place_of = first + lax.broadcasted_iota(jnp.int32, (512, lanes), 0)
                    shown = place_of <= within
                yield k_ref[rows, :], vt_ref[:, rows], shown

        def step(j, masked):
            for key, value, shown in pieces(j, masked):
                for u in range(heads):
                    top_ref[u], total_ref[u], acc_ref[u] = update(
                        u, key, value, shown, top_ref[u], total_ref[u], acc_ref[u]
                    )

        top_ref[...] = jnp.full_like(top_ref, FAR)
        total_ref[...] = jnp.zeros_like(total_ref)
        acc_ref[...] = jnp.zeros_like(acc_ref)

        def body(j, _):
            step(j, False)
            return 0

        lax.fori_loop(0, own, body, 0)
        step(own, True)
        alive = (own * stretch + within < length).astype(jnp.float32)
        for u in range(heads):
            out = (acc_ref[u, :HEAD_DIM] * (alive / acc_ref[u, HEAD_DIM : HEAD_DIM + 1])).T
            o_ref[:, u * HEAD_DIM : (u + 1) * HEAD_DIM] = out.astype(jnp.bfloat16)

    @pl.when(jnp.logical_not(live))
    def _():
        o_ref[...] = jnp.zeros_like(o_ref)

    @pl.when((block == pl.num_programs(1) - 1) & (turn == pl.num_programs(2) - 1))
    def _():
        for copy in copies:
            copy.wait()


def attend(stretch, tables, queries, keys, values):
    width = queries.shape[1]
    kv_width = keys.shape[1]
    local_kv = kv_width // HEAD_DIM
    group_size = width // kv_width
    heads = math.gcd(UNROLL, group_size)
    turns = group_size // heads
    lanes = math.gcd(ROW_BLOCK, stretch)
    span = MAX_STRETCHES * stretch
    cache = jax.ShapeDtypeStruct((span, kv_width), jnp.bfloat16)
    query_spec = pl.BlockSpec((lanes, heads * HEAD_DIM), lambda g, r, u, *_: (r, g * turns + u))
    kv_spec = pl.BlockSpec((keys.shape[0], HEAD_DIM), lambda g, r, u, *_: (0, g))
    return pl.pallas_call(
        functools.partial(attend_kernel, stretch, heads),
        out_shape=[jax.ShapeDtypeStruct((stretch, width), jnp.bfloat16), cache, cache],
        grid_spec=pltpu.PrefetchScalarGridSpec(
            num_scalar_prefetch=3,
            grid=(local_kv, stretch // lanes, turns),
            in_specs=[query_spec, kv_spec, kv_spec],
            out_specs=[query_spec] + [pl.BlockSpec(memory_space=pl.ANY)] * 2,
            scratch_shapes=[
                pltpu.VMEM((2, span, HEAD_DIM), jnp.bfloat16),
                pltpu.SemaphoreType.DMA((2,)),
                pltpu.VMEM((heads, 1, lanes), jnp.float32),
                pltpu.VMEM((heads, 1, lanes), jnp.float32),
                pltpu.VMEM((heads, HEAD_DIM + 16, lanes), jnp.float32),
                pltpu.VMEM((HEAD_DIM + 16, values.shape[0]), jnp.bfloat16),
            ],
        ),
        compiler_params=pltpu.CompilerParams(
            dimension_semantics=("arbitrary",) * 3, vmem_limit_bytes=48 * 2**20
        ),
        name="attend",
    )(*tables, queries, keys, values)


def gather_kernel(k_ref, v_ref, all_k, all_v, place_sem, send_sem, recv_sem):
    me = lax.axis_index("sp")
    rows = k_ref.shape[0]
    y, x, core = me // 4, me // 2 % 2, me % 2
    index = lambda y, x, core: y * 4 + x * 2 + core
    beside = index(y, 1 - x, core)
    above = index(1 - y, x, core)
    across = index(1 - y, 1 - x, core)
    partner = index(y, x, 1 - core)
    relay_from = core * beside + (1 - core) * above
    relay_to = core * above + (1 - core) * beside
    sources, outs = (k_ref, v_ref), (all_k, all_v)

    barrier = pltpu.get_barrier_semaphore()
    for other in (beside, above, partner):
        pl.semaphore_signal(barrier, inc=1, device_id={"sp": other}, device_id_type=MESH)
    pl.semaphore_wait(barrier, 3)

    def part(ref, owner):
        return ref.at[pl.ds(pl.multiple_of(owner * rows, rows), rows), :]

    def send(i, lane, source, owner, target):
        return pltpu.make_async_remote_copy(
            src_ref=source,
            dst_ref=part(outs[i], owner),
            send_sem=send_sem.at[lane, i],
            recv_sem=recv_sem.at[lane, i],
            device_id={"sp": target},
            device_id_type=MESH,
        )

    sent = []
    for i in range(2):
        for lane, target in ((0, beside), (1, above), (2, partner)):
            copy = send(i, lane, sources[i], me, target)
            copy.start()
            sent.append(copy)
        own = pltpu.make_async_copy(sources[i], part(outs[i], me), place_sem.at[i])
        own.start()
    relays = []
    for i in range(2):
        sent[3 * i].wait_recv()
        sent[3 * i + 1].wait_recv()
        relay = send(i, 3, part(outs[i], relay_from), relay_from, relay_to)
        relay.start()
        relays.append(relay)
        for lane, owner in ((4, beside), (5, above)):
            copy = send(i, lane, part(outs[i], owner), owner, partner)
            copy.start()
            relays.append(copy)
    last = []
    for i in range(2):
        relays[3 * i].wait_recv()
        copy = send(i, 6, part(outs[i], across), across, partner)
        copy.start()
        last.append(copy)
    for i in range(2):
        sent[3 * i + 2].wait_recv()
        relays[3 * i + 1].wait_recv()
        relays[3 * i + 2].wait_recv()
        last[i].wait_recv()
        pltpu.make_async_copy(sources[i], part(outs[i], me), place_sem.at[i]).wait()
    for copy in sent + relays + last:
        copy.wait_send()


def gather(keys, values):
    replicas = lax.axis_size("sp")
    if replicas != 8:
        return (
            lax.all_gather(keys, "sp", axis=0, tiled=True),
            lax.all_gather(values, "sp", axis=0, tiled=True),
        )
    shape = jax.ShapeDtypeStruct((replicas * keys.shape[0], keys.shape[1]), keys.dtype)
    return pl.pallas_call(
        gather_kernel,
        out_shape=[shape] * 2,
        in_specs=[pl.BlockSpec(memory_space=pltpu.VMEM)] * 2,
        out_specs=[pl.BlockSpec(memory_space=pl.ANY)] * 2,
        scratch_shapes=[
            pltpu.SemaphoreType.DMA((2,)),
            pltpu.SemaphoreType.DMA((7, 2)),
            pltpu.SemaphoreType.DMA((7, 2)),
        ],
        compiler_params=pltpu.CompilerParams(collective_id=0, has_side_effects=True),
        name="gather",
    )(keys, values)


def project_kernel(
    steps, a_ref, w_ref, o_ref, work, own, out_far, out_near, out_sum,
    in_far, in_near, in_sum, send_sem, recv_sem,
):
    me = lax.axis_index("tp")
    n = 4
    rows = a_ref.shape[0] // n
    step = pl.program_id(0)

    def hops(j):
        turn = 1 - 2 * (j % 2)
        return (me + turn + n) % n, (me - turn + n) % n

    def send(kind, j, target):
        source, dest = ((out_far, in_far), (out_near, in_near), (out_sum, in_sum))[kind]
        return pltpu.make_async_remote_copy(
            src_ref=source.at[j],
            dst_ref=dest.at[j],
            send_sem=send_sem.at[kind, j],
            recv_sem=recv_sem.at[kind, j],
            device_id={"tp": target},
            device_id_type=MESH,
        )

    @pl.when(step == 0)
    def _():
        barrier = pltpu.get_barrier_semaphore()
        for other in ((me + 1) % n, (me + n - 1) % n):
            pl.semaphore_signal(barrier, inc=1, device_id={"tp": other}, device_id_type=MESH)
        pl.semaphore_wait(barrier, 2)

    def rows_of(device):
        return pl.ds(pl.multiple_of(device * rows, rows), rows)

    def relay(j):
        toward, away = hops(j)
        send(0, j, toward).wait_recv()
        total = work[j % 2, rows_of(toward), :] + in_far[j].astype(jnp.float32)
        out_sum[j] = total.astype(jnp.bfloat16)
        send(2, j, toward).start()

    toward, away = hops(step)
    work[step % 2] = jnp.dot(a_ref[...], w_ref[...], preferred_element_type=jnp.float32)
    out_far[step] = work[step % 2, rows_of((me + 2) % n), :].astype(jnp.bfloat16)
    send(0, step, toward).start()
    out_near[step] = work[step % 2, rows_of(away), :].astype(jnp.bfloat16)
    send(1, step, away).start()
    own[step] = work[step % 2, rows_of(me), :]

    @pl.when(step > 0)
    def _():
        relay(step - 1)

    @pl.when(step == steps - 1)
    def _():
        relay(step)
        width = o_ref.shape[1] // steps
        for j in range(steps):
            toward, away = hops(j)
            send(1, j, away).wait_recv()
            send(2, j, toward).wait_recv()
            total = own[j] + in_near[j].astype(jnp.float32) + in_sum[j].astype(jnp.float32)
            o_ref[:, j * width : (j + 1) * width] = total.astype(jnp.bfloat16)
        for j in range(steps):
            toward, away = hops(j)
            send(0, j, toward).wait_send()
            send(1, j, away).wait_send()
            send(2, j, toward).wait_send()


def project(attended, w_out):
    if lax.axis_size("tp") != 4:
        partial = jnp.dot(attended, w_out, preferred_element_type=jnp.float32)
        return lax.psum_scatter(
            partial.astype(jnp.bfloat16), "tp", scatter_dimension=0, tiled=True
        )
    tokens, depth = attended.shape
    features = w_out.shape[1]
    rows = tokens // 4
    steps = 8
    width = features // steps
    buffer = pltpu.VMEM((steps, rows, width), jnp.bfloat16)
    return pl.pallas_call(
        functools.partial(project_kernel, steps),
        out_shape=jax.ShapeDtypeStruct((rows, features), jnp.bfloat16),
        grid=(steps,),
        in_specs=[
            pl.BlockSpec((tokens, depth), lambda j: (0, 0)),
            pl.BlockSpec((depth, width), lambda j: (0, j)),
        ],
        out_specs=pl.BlockSpec((rows, features), lambda j: (0, 0)),
        scratch_shapes=[
            pltpu.VMEM((2, tokens, width), jnp.float32),
            pltpu.VMEM((steps, rows, width), jnp.float32),
            buffer, buffer, buffer, buffer, buffer, buffer,
            pltpu.SemaphoreType.DMA((3, steps)),
            pltpu.SemaphoreType.DMA((3, steps)),
        ],
        compiler_params=pltpu.CompilerParams(
            collective_id=1,
            has_side_effects=True,
            dimension_semantics=("arbitrary",),
            vmem_limit_bytes=48 * 2**20,
        ),
        name="project",
    )(attended, w_out)


def shards(queries, keys, values, w_out, lengths, stretch_owner, home_replica):
    stretch = queries.shape[0]
    tables = (stretch_owner, lengths, home_replica)
    all_keys, all_values = gather(keys, values)
    attended, kept_keys, kept_values = attend(stretch, tables, queries, all_keys, all_values)
    return (project(attended, w_out), kept_keys, kept_values)


def solution(mesh):
    placed = (P("sp", "tp"), P("sp", "tp"), P("sp", "tp"), P("tp", None), P(), P(), P())
    return jax.shard_map(
        shards,
        mesh=mesh,
        in_specs=placed,
        out_specs=(P(("sp", "tp"), None), P("sp", "tp"), P("sp", "tp")),
        check_vma=False,
    )
```

```python
import functools
import math

import jax
import jax.numpy as jnp
from jax import lax
from jax.experimental import pallas as pl
from jax.experimental.pallas import tpu as pltpu
from jax.sharding import PartitionSpec as P

HEAD_DIM = 128
MAX_STRETCHES = 8
ROW_BLOCK = 512
UNROLL = 4
LOG2E = math.log2(math.e)
FAR = -1e30
MESH = pl.DeviceIdType.MESH


def find(table, value):
    index = jnp.int32(0)
    for j in range(table.shape[0]):
        index = index + jnp.where(table[j] == value, j, 0)
    return index


def attend_kernel(
    stretch, heads, owner_ref, length_ref, home_ref, q_ref, k_ref, v_ref, o_ref, kc_ref, vc_ref,
    stage, sems, top_ref, high_ref, acc_ref, vt_ref, score_ref,
):
    me = lax.axis_index("sp")
    mine = find(owner_ref, me)
    prompt = mine // MAX_STRETCHES
    own = mine % MAX_STRETCHES
    length = length_ref[prompt]
    lanes = q_ref.shape[0]
    group, block, turn = pl.program_id(0), pl.program_id(1), pl.program_id(2)
    columns = pl.ds(pl.multiple_of(group * HEAD_DIM, HEAD_DIM), HEAD_DIM)
    copies = [
        pltpu.make_async_copy(stage.at[i], out.at[:, columns], sems.at[i])
        for i, out in enumerate((kc_ref, vc_ref))
    ]

    @pl.when((block == 0) & (turn == 0))
    def _():
        homed = jnp.int32(0)
        kept = jnp.int32(0)
        for p in range(home_ref.shape[0]):
            here = home_ref[p] == me
            homed = jnp.where(here, p, homed)
            kept = jnp.where(here, length_ref[p], kept)

        def fill(j, _):
            start = pl.multiple_of(owner_ref[homed * MAX_STRETCHES + j] * stretch, stretch)
            target = pl.ds(pl.multiple_of(j * stretch, stretch), stretch)
            position = j * stretch + lax.broadcasted_iota(jnp.int32, (stretch, HEAD_DIM), 0)
            for i, source in enumerate((k_ref, v_ref)):
                block = source[pl.ds(start, stretch), :]
                stage[i, target, :] = jnp.where(position < kept, block, jnp.zeros_like(block))
            return 0

        lax.fori_loop(0, MAX_STRETCHES, fill, 0)
        for copy in copies:
            copy.start()

        def turned(j, _):
            rows = pl.ds(pl.multiple_of(j * stretch, stretch), stretch)
            vt_ref[:HEAD_DIM, rows] = v_ref[rows, :].T
            return 0

        lax.fori_loop(0, v_ref.shape[0] // stretch, turned, 0)
        vt_ref[HEAD_DIM:, :] = jnp.ones((16, v_ref.shape[0]), jnp.bfloat16)

    within = block * lanes + lax.broadcasted_iota(jnp.int32, (1, lanes), 1)
    live = own * stretch + block * lanes < length

    @pl.when(live)
    def _():
        scale = HEAD_DIM ** (-0.5) * LOG2E
        piece = stretch // 2

        def first_row(j):
            return pl.multiple_of(owner_ref[prompt * MAX_STRETCHES + j] * stretch, stretch)

        def score(j, u, c):
            rows = pl.ds(first_row(j) + c * piece, piece)
            query = q_ref[:, u * HEAD_DIM : (u + 1) * HEAD_DIM]
            scores = lax.dot_general(
                k_ref[rows, :], query, (((1,), (1,)), ((), ())), preferred_element_type=jnp.float32
            )
            score_ref[u, c * piece : (c + 1) * piece, :] = scores
            return jnp.max(scores, axis=0, keepdims=True)

        def score_all(j, u):
            highest = [score(j, u, c) for c in range(2)]
            high_ref[u] = functools.reduce(jnp.maximum, highest)

        def spread(j, u, masked, ahead):
            top = top_ref[u]
            start = first_row(j)
            if masked:
                def seen(c):
                    place_of = c * piece + lax.broadcasted_iota(jnp.int32, (piece, lanes), 0)
                    part = score_ref[u, c * piece : (c + 1) * piece, :]
                    return jnp.where(place_of <= within, part, FAR)

                high = functools.reduce(
                    jnp.maximum,
                    [jnp.max(seen(c), axis=0, keepdims=True) for c in range(2)],
                )
            else:
                def seen(c):
                    return score_ref[u, c * piece : (c + 1) * piece, :]

                high = high_ref[u]
            new_top = jnp.maximum(top, high * scale)
            rescale = jnp.exp2(top - new_top)
            highest, weights = [], []
            acc = acc_ref[u] * rescale
            for c in range(2):
                if ahead is not None:
                    highest.append(score(ahead[0], ahead[1], c))
                weights.append(jnp.exp2(seen(c) * scale - new_top).astype(jnp.bfloat16))
            acc = acc + jnp.dot(
                vt_ref[:, pl.ds(start, stretch)], jnp.concatenate(weights, axis=0),
                preferred_element_type=jnp.float32,
            )
            acc_ref[u] = acc
            top_ref[u] = new_top
            if ahead is not None:
                high_ref[ahead[1]] = functools.reduce(jnp.maximum, highest)

        top_ref[...] = jnp.full_like(top_ref, FAR)
        acc_ref[...] = jnp.zeros_like(acc_ref)
        score_all(0, 0)

        def body(j, _):
            for u in range(heads):
                spread(j, u, False, (j, u + 1) if u + 1 < heads else (j + 1, 0))
            return 0

        lax.fori_loop(0, own, body, 0)
        for u in range(heads):
            spread(own, u, True, (own, u + 1) if u + 1 < heads else None)
        alive = (own * stretch + within < length).astype(jnp.float32)
        for u in range(heads):
            out = (acc_ref[u, :HEAD_DIM] * (alive / acc_ref[u, HEAD_DIM : HEAD_DIM + 1])).T
            o_ref[:, u * HEAD_DIM : (u + 1) * HEAD_DIM] = out.astype(jnp.bfloat16)

    @pl.when(jnp.logical_not(live))
    def _():
        o_ref[...] = jnp.zeros_like(o_ref)

    @pl.when((block == pl.num_programs(1) - 1) & (turn == pl.num_programs(2) - 1))
    def _():
        for copy in copies:
            copy.wait()


def attend(stretch, tables, queries, keys, values):
    width = queries.shape[1]
    kv_width = keys.shape[1]
    local_kv = kv_width // HEAD_DIM
    group_size = width // kv_width
    heads = math.gcd(UNROLL, group_size)
    turns = group_size // heads
    lanes = math.gcd(ROW_BLOCK, stretch)
    span = MAX_STRETCHES * stretch
    cache = jax.ShapeDtypeStruct((span, kv_width), jnp.bfloat16)
    query_spec = pl.BlockSpec((lanes, heads * HEAD_DIM), lambda g, r, u, *_: (r, g * turns + u))
    kv_spec = pl.BlockSpec((keys.shape[0], HEAD_DIM), lambda g, r, u, *_: (0, g))
    return pl.pallas_call(
        functools.partial(attend_kernel, stretch, heads),
        out_shape=[jax.ShapeDtypeStruct((stretch, width), jnp.bfloat16), cache, cache],
        grid_spec=pltpu.PrefetchScalarGridSpec(
            num_scalar_prefetch=3,
            grid=(local_kv, stretch // lanes, turns),
            in_specs=[query_spec, kv_spec, kv_spec],
            out_specs=[query_spec] + [pl.BlockSpec(memory_space=pl.ANY)] * 2,
            scratch_shapes=[
                pltpu.VMEM((2, span, HEAD_DIM), jnp.bfloat16),
                pltpu.SemaphoreType.DMA((2,)),
                pltpu.VMEM((heads, 1, lanes), jnp.float32),
                pltpu.VMEM((heads, 1, lanes), jnp.float32),
                pltpu.VMEM((heads, HEAD_DIM + 16, lanes), jnp.float32),
                pltpu.VMEM((HEAD_DIM + 16, values.shape[0]), jnp.bfloat16),
                pltpu.VMEM((heads, stretch, lanes), jnp.float32),
            ],
        ),
        compiler_params=pltpu.CompilerParams(
            dimension_semantics=("arbitrary",) * 3, vmem_limit_bytes=48 * 2**20
        ),
        name="attend",
    )(*tables, queries, keys, values)


def gather_kernel(k_ref, v_ref, all_k, all_v, place_sem, send_sem, recv_sem):
    me = lax.axis_index("sp")
    rows = k_ref.shape[0]
    y, x, core = me // 4, me // 2 % 2, me % 2
    index = lambda y, x, core: y * 4 + x * 2 + core
    beside = index(y, 1 - x, core)
    above = index(1 - y, x, core)
    across = index(1 - y, 1 - x, core)
    partner = index(y, x, 1 - core)
    relay_from = core * beside + (1 - core) * above
    relay_to = core * above + (1 - core) * beside
    sources, outs = (k_ref, v_ref), (all_k, all_v)

    barrier = pltpu.get_barrier_semaphore()
    for other in (beside, above, partner):
        pl.semaphore_signal(barrier, inc=1, device_id={"sp": other}, device_id_type=MESH)
    pl.semaphore_wait(barrier, 3)

    def part(ref, owner):
        return ref.at[pl.ds(pl.multiple_of(owner * rows, rows), rows), :]

    def send(i, lane, source, owner, target):
        return pltpu.make_async_remote_copy(
            src_ref=source,
            dst_ref=part(outs[i], owner),
            send_sem=send_sem.at[lane, i],
            recv_sem=recv_sem.at[lane, i],
            device_id={"sp": target},
            device_id_type=MESH,
        )

    sent = []
    for i in range(2):
        for lane, target in ((0, beside), (1, above), (2, partner)):
            copy = send(i, lane, sources[i], me, target)
            copy.start()
            sent.append(copy)
        own = pltpu.make_async_copy(sources[i], part(outs[i], me), place_sem.at[i])
        own.start()
    relays = []
    for i in range(2):
        sent[3 * i].wait_recv()
        sent[3 * i + 1].wait_recv()
        relay = send(i, 3, part(outs[i], relay_from), relay_from, relay_to)
        relay.start()
        relays.append(relay)
        for lane, owner in ((4, beside), (5, above)):
            copy = send(i, lane, part(outs[i], owner), owner, partner)
            copy.start()
            relays.append(copy)
    last = []
    for i in range(2):
        relays[3 * i].wait_recv()
        copy = send(i, 6, part(outs[i], across), across, partner)
        copy.start()
        last.append(copy)
    for i in range(2):
        sent[3 * i + 2].wait_recv()
        relays[3 * i + 1].wait_recv()
        relays[3 * i + 2].wait_recv()
        last[i].wait_recv()
        pltpu.make_async_copy(sources[i], part(outs[i], me), place_sem.at[i]).wait()
    for copy in sent + relays + last:
        copy.wait_send()


def gather(keys, values):
    replicas = lax.axis_size("sp")
    if replicas != 8:
        return (
            lax.all_gather(keys, "sp", axis=0, tiled=True),
            lax.all_gather(values, "sp", axis=0, tiled=True),
        )
    shape = jax.ShapeDtypeStruct((replicas * keys.shape[0], keys.shape[1]), keys.dtype)
    return pl.pallas_call(
        gather_kernel,
        out_shape=[shape] * 2,
        in_specs=[pl.BlockSpec(memory_space=pltpu.VMEM)] * 2,
        out_specs=[pl.BlockSpec(memory_space=pl.ANY)] * 2,
        scratch_shapes=[
            pltpu.SemaphoreType.DMA((2,)),
            pltpu.SemaphoreType.DMA((7, 2)),
            pltpu.SemaphoreType.DMA((7, 2)),
        ],
        compiler_params=pltpu.CompilerParams(collective_id=0, has_side_effects=True),
        name="gather",
    )(keys, values)


def project_kernel(
    steps, a_ref, w_ref, o_ref, work, own, out_far, out_near, out_sum,
    in_far, in_near, in_sum, send_sem, recv_sem,
):
    me = lax.axis_index("tp")
    n = 4
    rows = a_ref.shape[0] // n
    step = pl.program_id(0)

    def hops(j):
        turn = 1 - 2 * (j % 2)
        return (me + turn + n) % n, (me - turn + n) % n

    def send(kind, j, target):
        source, dest = ((out_far, in_far), (out_near, in_near), (out_sum, in_sum))[kind]
        return pltpu.make_async_remote_copy(
            src_ref=source.at[j],
            dst_ref=dest.at[j],
            send_sem=send_sem.at[kind, j],
            recv_sem=recv_sem.at[kind, j],
            device_id={"tp": target},
            device_id_type=MESH,
        )

    @pl.when(step == 0)
    def _():
        barrier = pltpu.get_barrier_semaphore()
        for other in ((me + 1) % n, (me + n - 1) % n):
            pl.semaphore_signal(barrier, inc=1, device_id={"tp": other}, device_id_type=MESH)
        pl.semaphore_wait(barrier, 2)

    def rows_of(device):
        return pl.ds(pl.multiple_of(device * rows, rows), rows)

    def relay(j):
        toward, away = hops(j)
        send(0, j, toward).wait_recv()
        total = work[j % 2, rows_of(toward), :] + in_far[j].astype(jnp.float32)
        out_sum[j] = total.astype(jnp.bfloat16)
        send(2, j, toward).start()

    toward, away = hops(step)
    work[step % 2] = jnp.dot(a_ref[...], w_ref[...], preferred_element_type=jnp.float32)
    out_far[step] = work[step % 2, rows_of((me + 2) % n), :].astype(jnp.bfloat16)
    send(0, step, toward).start()
    out_near[step] = work[step % 2, rows_of(away), :].astype(jnp.bfloat16)
    send(1, step, away).start()
    own[step] = work[step % 2, rows_of(me), :]

    @pl.when(step > 0)
    def _():
        relay(step - 1)

    @pl.when(step == steps - 1)
    def _():
        relay(step)
        width = o_ref.shape[1] // steps
        for j in range(steps):
            toward, away = hops(j)
            send(1, j, away).wait_recv()
            send(2, j, toward).wait_recv()
            total = own[j] + in_near[j].astype(jnp.float32) + in_sum[j].astype(jnp.float32)
            o_ref[:, j * width : (j + 1) * width] = total.astype(jnp.bfloat16)
        for j in range(steps):
            toward, away = hops(j)
            send(0, j, toward).wait_send()
            send(1, j, away).wait_send()
            send(2, j, toward).wait_send()


def project(attended, w_out):
    if lax.axis_size("tp") != 4:
        partial = jnp.dot(attended, w_out, preferred_element_type=jnp.float32)
        return lax.psum_scatter(
            partial.astype(jnp.bfloat16), "tp", scatter_dimension=0, tiled=True
        )
    tokens, depth = attended.shape
    features = w_out.shape[1]
    rows = tokens // 4
    steps = 8
    width = features // steps
    buffer = pltpu.VMEM((steps, rows, width), jnp.bfloat16)
    return pl.pallas_call(
        functools.partial(project_kernel, steps),
        out_shape=jax.ShapeDtypeStruct((rows, features), jnp.bfloat16),
        grid=(steps,),
        in_specs=[
            pl.BlockSpec((tokens, depth), lambda j: (0, 0)),
            pl.BlockSpec((depth, width), lambda j: (0, j)),
        ],
        out_specs=pl.BlockSpec((rows, features), lambda j: (0, 0)),
        scratch_shapes=[
            pltpu.VMEM((2, tokens, width), jnp.float32),
            pltpu.VMEM((steps, rows, width), jnp.float32),
            buffer, buffer, buffer, buffer, buffer, buffer,
            pltpu.SemaphoreType.DMA((3, steps)),
            pltpu.SemaphoreType.DMA((3, steps)),
        ],
        compiler_params=pltpu.CompilerParams(
            collective_id=1,
            has_side_effects=True,
            dimension_semantics=("arbitrary",),
            vmem_limit_bytes=48 * 2**20,
        ),
        name="project",
    )(attended, w_out)


def shards(queries, keys, values, w_out, lengths, stretch_owner, home_replica):
    stretch = queries.shape[0]
    tables = (stretch_owner, lengths, home_replica)
    all_keys, all_values = gather(keys, values)
    attended, kept_keys, kept_values = attend(stretch, tables, queries, all_keys, all_values)
    return (project(attended, w_out), kept_keys, kept_values)


def solution(mesh):
    placed = (P("sp", "tp"), P("sp", "tp"), P("sp", "tp"), P("tp", None), P(), P(), P())
    return jax.shard_map(
        shards,
        mesh=mesh,
        in_specs=placed,
        out_specs=(P(("sp", "tp"), None), P("sp", "tp"), P("sp", "tp")),
        check_vma=False,
    )
```

```python
import functools
import math

import jax
import jax.numpy as jnp
from jax import lax
from jax.experimental import pallas as pl
from jax.experimental.pallas import tpu as pltpu
from jax.sharding import PartitionSpec as P

HEAD_DIM = 128
MAX_STRETCHES = 8
ROW_BLOCK = 512
UNROLL = 4
LOG2E = math.log2(math.e)
FAR = -1e30
MESH = pl.DeviceIdType.MESH


def find(table, value):
    index = jnp.int32(0)
    for j in range(table.shape[0]):
        index = index + jnp.where(table[j] == value, j, 0)
    return index


def attend_kernel(
    stretch, heads, owner_ref, length_ref, home_ref, q_ref, k_ref, v_ref, o_ref, kc_ref, vc_ref,
    stage, sems, top_ref, high_ref, acc_ref, vt_ref, score_ref,
):
    me = lax.axis_index("sp")
    mine = find(owner_ref, me)
    prompt = mine // MAX_STRETCHES
    own = mine % MAX_STRETCHES
    length = length_ref[prompt]
    lanes = q_ref.shape[0]
    group, block, turn = pl.program_id(0), pl.program_id(1), pl.program_id(2)
    columns = pl.ds(pl.multiple_of(group * HEAD_DIM, HEAD_DIM), HEAD_DIM)
    copies = [
        pltpu.make_async_copy(stage.at[i], out.at[:, columns], sems.at[i])
        for i, out in enumerate((kc_ref, vc_ref))
    ]

    @pl.when((block == 0) & (turn == 0))
    def _():
        homed = jnp.int32(0)
        kept = jnp.int32(0)
        for p in range(home_ref.shape[0]):
            here = home_ref[p] == me
            homed = jnp.where(here, p, homed)
            kept = jnp.where(here, length_ref[p], kept)

        def fill(j, _):
            start = pl.multiple_of(owner_ref[homed * MAX_STRETCHES + j] * stretch, stretch)
            target = pl.ds(pl.multiple_of(j * stretch, stretch), stretch)
            position = j * stretch + lax.broadcasted_iota(jnp.int32, (stretch, HEAD_DIM), 0)
            for i, source in enumerate((k_ref, v_ref)):
                block = source[pl.ds(start, stretch), :]
                stage[i, target, :] = jnp.where(position < kept, block, jnp.zeros_like(block))
            return 0

        lax.fori_loop(0, MAX_STRETCHES, fill, 0)
        for copy in copies:
            copy.start()

        def turned(j, _):
            rows = pl.ds(pl.multiple_of(j * stretch, stretch), stretch)
            vt_ref[:HEAD_DIM, rows] = v_ref[rows, :].T
            return 0

        lax.fori_loop(0, v_ref.shape[0] // stretch, turned, 0)
        vt_ref[HEAD_DIM:, :] = jnp.ones((16, v_ref.shape[0]), jnp.bfloat16)

    within = block * lanes + lax.broadcasted_iota(jnp.int32, (1, lanes), 1)
    live = own * stretch + block * lanes < length

    @pl.when(live)
    def _():
        scale = HEAD_DIM ** (-0.5) * LOG2E
        piece = stretch // 2

        def first_row(j):
            return pl.multiple_of(owner_ref[prompt * MAX_STRETCHES + j] * stretch, stretch)

        def score(j, u, c):
            rows = pl.ds(first_row(j) + c * piece, piece)
            query = q_ref[:, u * HEAD_DIM : (u + 1) * HEAD_DIM]
            scores = lax.dot_general(
                k_ref[rows, :], query, (((1,), (1,)), ((), ())), preferred_element_type=jnp.float32
            )
            score_ref[u, c * piece : (c + 1) * piece, :] = scores
            return jnp.max(scores, axis=0, keepdims=True)

        def score_all(j, u):
            highest = [score(j, u, c) for c in range(2)]
            high_ref[u] = functools.reduce(jnp.maximum, highest)

        def spread(j, u, masked, ahead):
            top = top_ref[u]
            start = first_row(j)
            if masked:
                def seen(c):
                    place_of = c * piece + lax.broadcasted_iota(jnp.int32, (piece, lanes), 0)
                    part = score_ref[u, c * piece : (c + 1) * piece, :]
                    return jnp.where(place_of <= within, part, FAR)

                high = functools.reduce(
                    jnp.maximum,
                    [jnp.max(seen(c), axis=0, keepdims=True) for c in range(2)],
                )
            else:
                def seen(c):
                    return score_ref[u, c * piece : (c + 1) * piece, :]

                high = high_ref[u]
            new_top = jnp.maximum(top, high * scale)
            rescale = jnp.exp2(top - new_top)
            highest, weights = [], []
            acc = acc_ref[u] * rescale
            for c in range(2):
                if ahead is not None:
                    highest.append(score(ahead[0], ahead[1], c))
                weights.append(jnp.exp2(seen(c) * scale - new_top).astype(jnp.bfloat16))
            acc = acc + jnp.dot(
                vt_ref[:, pl.ds(start, stretch)], jnp.concatenate(weights, axis=0),
                preferred_element_type=jnp.float32,
            )
            acc_ref[u] = acc
            top_ref[u] = new_top
            if ahead is not None:
                high_ref[ahead[1]] = functools.reduce(jnp.maximum, highest)

        top_ref[...] = jnp.full_like(top_ref, FAR)
        acc_ref[...] = jnp.zeros_like(acc_ref)
        score_all(0, 0)

        def body(j, _):
            for u in range(heads):
                spread(j, u, False, (j, u + 1) if u + 1 < heads else (j + 1, 0))
            return 0

        lax.fori_loop(0, own, body, 0)
        for u in range(heads):
            spread(own, u, True, (own, u + 1) if u + 1 < heads else None)
        alive = (own * stretch + within < length).astype(jnp.float32)
        for u in range(heads):
            out = (acc_ref[u, :HEAD_DIM] * (alive / acc_ref[u, HEAD_DIM : HEAD_DIM + 1])).T
            o_ref[:, u * HEAD_DIM : (u + 1) * HEAD_DIM] = out.astype(jnp.bfloat16)

    @pl.when(jnp.logical_not(live))
    def _():
        o_ref[...] = jnp.zeros_like(o_ref)

    @pl.when((block == pl.num_programs(1) - 1) & (turn == pl.num_programs(2) - 1))
    def _():
        for copy in copies:
            copy.wait()


def attend(stretch, tables, queries, keys, values):
    width = queries.shape[1]
    kv_width = keys.shape[1]
    local_kv = kv_width // HEAD_DIM
    group_size = width // kv_width
    heads = math.gcd(UNROLL, group_size)
    turns = group_size // heads
    lanes = math.gcd(ROW_BLOCK, stretch)
    span = MAX_STRETCHES * stretch
    cache = jax.ShapeDtypeStruct((span, kv_width), jnp.bfloat16)
    query_spec = pl.BlockSpec((lanes, heads * HEAD_DIM), lambda g, r, u, *_: (r, g * turns + u))
    kv_spec = pl.BlockSpec((keys.shape[0], HEAD_DIM), lambda g, r, u, *_: (0, g))
    return pl.pallas_call(
        functools.partial(attend_kernel, stretch, heads),
        out_shape=[jax.ShapeDtypeStruct((stretch, width), jnp.bfloat16), cache, cache],
        grid_spec=pltpu.PrefetchScalarGridSpec(
            num_scalar_prefetch=3,
            grid=(local_kv, stretch // lanes, turns),
            in_specs=[query_spec, kv_spec, kv_spec],
            out_specs=[query_spec] + [pl.BlockSpec(memory_space=pl.ANY)] * 2,
            scratch_shapes=[
                pltpu.VMEM((2, span, HEAD_DIM), jnp.bfloat16),
                pltpu.SemaphoreType.DMA((2,)),
                pltpu.VMEM((heads, 1, lanes), jnp.float32),
                pltpu.VMEM((heads, 1, lanes), jnp.float32),
                pltpu.VMEM((heads, HEAD_DIM + 16, lanes), jnp.float32),
                pltpu.VMEM((HEAD_DIM + 16, values.shape[0]), jnp.bfloat16),
                pltpu.VMEM((heads, stretch, lanes), jnp.float32),
            ],
        ),
        compiler_params=pltpu.CompilerParams(
            dimension_semantics=("arbitrary",) * 3, vmem_limit_bytes=48 * 2**20
        ),
        name="attend",
    )(*tables, queries, keys, values)


def gather_kernel(k_ref, v_ref, all_k, all_v, place_sem, send_sem, recv_sem):
    me = lax.axis_index("sp")
    rows = k_ref.shape[0]
    y, x, core = me // 4, me // 2 % 2, me % 2
    index = lambda y, x, core: y * 4 + x * 2 + core
    beside = index(y, 1 - x, core)
    above = index(1 - y, x, core)
    across = index(1 - y, 1 - x, core)
    partner = index(y, x, 1 - core)
    relay_from = core * beside + (1 - core) * above
    relay_to = core * above + (1 - core) * beside
    sources, outs = (k_ref, v_ref), (all_k, all_v)

    barrier = pltpu.get_barrier_semaphore()
    for other in (beside, above, partner):
        pl.semaphore_signal(barrier, inc=1, device_id={"sp": other}, device_id_type=MESH)
    pl.semaphore_wait(barrier, 3)

    def part(ref, owner):
        return ref.at[pl.ds(pl.multiple_of(owner * rows, rows), rows), :]

    def send(i, lane, source, owner, target):
        return pltpu.make_async_remote_copy(
            src_ref=source,
            dst_ref=part(outs[i], owner),
            send_sem=send_sem.at[lane, i],
            recv_sem=recv_sem.at[lane, i],
            device_id={"sp": target},
            device_id_type=MESH,
        )

    sent = []
    for i in range(2):
        for lane, target in ((0, beside), (1, above), (2, partner)):
            copy = send(i, lane, sources[i], me, target)
            copy.start()
            sent.append(copy)
        own = pltpu.make_async_copy(sources[i], part(outs[i], me), place_sem.at[i])
        own.start()
    relays = []
    for i in range(2):
        sent[3 * i].wait_recv()
        sent[3 * i + 1].wait_recv()
        relay = send(i, 3, part(outs[i], relay_from), relay_from, relay_to)
        relay.start()
        relays.append(relay)
        for lane, owner in ((4, beside), (5, above)):
            copy = send(i, lane, part(outs[i], owner), owner, partner)
            copy.start()
            relays.append(copy)
    last = []
    for i in range(2):
        relays[3 * i].wait_recv()
        copy = send(i, 6, part(outs[i], across), across, partner)
        copy.start()
        last.append(copy)
    for i in range(2):
        sent[3 * i + 2].wait_recv()
        relays[3 * i + 1].wait_recv()
        relays[3 * i + 2].wait_recv()
        last[i].wait_recv()
        pltpu.make_async_copy(sources[i], part(outs[i], me), place_sem.at[i]).wait()
    for copy in sent + relays + last:
        copy.wait_send()


def gather(keys, values):
    replicas = lax.axis_size("sp")
    if replicas != 8:
        return (
            lax.all_gather(keys, "sp", axis=0, tiled=True),
            lax.all_gather(values, "sp", axis=0, tiled=True),
        )
    shape = jax.ShapeDtypeStruct((replicas * keys.shape[0], keys.shape[1]), keys.dtype)
    return pl.pallas_call(
        gather_kernel,
        out_shape=[shape] * 2,
        in_specs=[pl.BlockSpec(memory_space=pltpu.VMEM)] * 2,
        out_specs=[pl.BlockSpec(memory_space=pl.ANY)] * 2,
        scratch_shapes=[
            pltpu.SemaphoreType.DMA((2,)),
            pltpu.SemaphoreType.DMA((7, 2)),
            pltpu.SemaphoreType.DMA((7, 2)),
        ],
        compiler_params=pltpu.CompilerParams(collective_id=0, has_side_effects=True),
        name="gather",
    )(keys, values)


def project_kernel(
    steps, a_ref, w_ref, o_ref, work, own, out, from_left, from_right, send_sem, left_sem, right_sem
):
    me = lax.axis_index("tp")
    n = 4
    rows = a_ref.shape[0] // n
    step = pl.program_id(0)

    def push(j, part, up):
        return pltpu.make_async_remote_copy(
            src_ref=out.at[j, part],
            dst_ref=(from_left if up else from_right).at[j, part],
            send_sem=send_sem.at[j, part],
            recv_sem=(left_sem if up else right_sem).at[j, part],
            device_id={"tp": (me + 1) % n if up else (me + n - 1) % n},
            device_id_type=MESH,
        )

    @pl.when(step == 0)
    def _():
        barrier = pltpu.get_barrier_semaphore()
        for other in ((me + 1) % n, (me + n - 1) % n):
            pl.semaphore_signal(barrier, inc=1, device_id={"tp": other}, device_id_type=MESH)
        pl.semaphore_wait(barrier, 2)

    def piece(j, part):
        return work[j % 2, part * rows : (part + 1) * rows, :]

    def relay(j, up):
        for part in range(n - 1, 1, -1) if up else range(n - 2):

            @pl.when((me < part) if up else (me > part))
            def _():
                push(j, part, up).wait_recv()
                before = (from_left if up else from_right)[j, part]
                out[j, part] = (piece(j, part) + before.astype(jnp.float32)).astype(jnp.bfloat16)
                push(j, part, up).start()

    def relays(j):
        @pl.when((me > 0) & (2 * me < n))
        def _():
            relay(j, True)
            relay(j, False)

        @pl.when((me < n - 1) & (2 * me >= n))
        def _():
            relay(j, False)
            relay(j, True)

    work[step % 2] = jnp.dot(a_ref[...], w_ref[...], preferred_element_type=jnp.float32)
    own[step] = work[step % 2, pl.ds(pl.multiple_of(me * rows, rows), rows), :]

    @pl.when(me == 0)
    def _():
        for part in range(n - 1, 0, -1):
            out[step, part] = piece(step, part).astype(jnp.bfloat16)
            push(step, part, True).start()

    @pl.when(me == n - 1)
    def _():
        for part in range(n - 1):
            out[step, part] = piece(step, part).astype(jnp.bfloat16)
            push(step, part, False).start()

    @pl.when(step > 0)
    def _():
        relays(step - 1)

    @pl.when(step == steps - 1)
    def _():
        relays(step)

        @pl.when(me > 0)
        def _():
            for j in range(steps):
                push(j, me, True).wait_recv()
                own[j] = own[j] + from_left[j, me].astype(jnp.float32)

        @pl.when(me < n - 1)
        def _():
            for j in range(steps):
                push(j, me, False).wait_recv()
                own[j] = own[j] + from_right[j, me].astype(jnp.float32)

        width = o_ref.shape[1] // steps
        for j in range(steps):
            o_ref[:, j * width : (j + 1) * width] = own[j].astype(jnp.bfloat16)
        for part in range(n):

            @pl.when(me < part)
            def _():
                for j in range(steps):
                    push(j, part, True).wait_send()

            @pl.when(me > part)
            def _():
                for j in range(steps):
                    push(j, part, False).wait_send()


def project(attended, w_out):
    if lax.axis_size("tp") != 4:
        partial = jnp.dot(attended, w_out, preferred_element_type=jnp.float32)
        return lax.psum_scatter(
            partial.astype(jnp.bfloat16), "tp", scatter_dimension=0, tiled=True
        )
    tokens, depth = attended.shape
    features = w_out.shape[1]
    rows = tokens // 4
    steps = 8
    width = features // steps
    buffer = pltpu.VMEM((steps, 4, rows, width), jnp.bfloat16)
    return pl.pallas_call(
        functools.partial(project_kernel, steps),
        out_shape=jax.ShapeDtypeStruct((rows, features), jnp.bfloat16),
        grid=(steps,),
        in_specs=[
            pl.BlockSpec((tokens, depth), lambda j: (0, 0)),
            pl.BlockSpec((depth, width), lambda j: (0, j)),
        ],
        out_specs=pl.BlockSpec((rows, features), lambda j: (0, 0)),
        scratch_shapes=[
            pltpu.VMEM((2, tokens, width), jnp.float32),
            pltpu.VMEM((steps, rows, width), jnp.float32),
            buffer, buffer, buffer,
            pltpu.SemaphoreType.DMA((steps, 4)),
            pltpu.SemaphoreType.DMA((steps, 4)),
            pltpu.SemaphoreType.DMA((steps, 4)),
        ],
        compiler_params=pltpu.CompilerParams(
            collective_id=1,
            has_side_effects=True,
            dimension_semantics=("arbitrary",),
            vmem_limit_bytes=48 * 2**20,
        ),
        name="project",
    )(attended, w_out)


def shards(queries, keys, values, w_out, lengths, stretch_owner, home_replica):
    stretch = queries.shape[0]
    tables = (stretch_owner, lengths, home_replica)
    all_keys, all_values = gather(keys, values)
    attended, kept_keys, kept_values = attend(stretch, tables, queries, all_keys, all_values)
    return (project(attended, w_out), kept_keys, kept_values)


def solution(mesh):
    placed = (P("sp", "tp"), P("sp", "tp"), P("sp", "tp"), P("tp", None), P(), P(), P())
    return jax.shard_map(
        shards,
        mesh=mesh,
        in_specs=placed,
        out_specs=(P(("sp", "tp"), None), P("sp", "tp"), P("sp", "tp")),
        check_vma=False,
    )
```

```python
import functools
import math

import jax
import jax.numpy as jnp
from jax import lax
from jax.experimental import pallas as pl
from jax.experimental.pallas import tpu as pltpu
from jax.sharding import PartitionSpec as P

HEAD_DIM = 128
MAX_STRETCHES = 8
ROW_BLOCK = 512
UNROLL = 4
LOG2E = math.log2(math.e)
FAR = -1e30
MESH = pl.DeviceIdType.MESH


def find(table, value):
    index = jnp.int32(0)
    for j in range(table.shape[0]):
        index = index + jnp.where(table[j] == value, j, 0)
    return index


def attend_kernel(
    stretch, heads, owner_ref, length_ref, home_ref, q_ref, k_ref, v_ref, o_ref, kc_ref, vc_ref,
    stage, sems, top_ref, high_ref, acc_ref, vt_ref, score_ref,
):
    me = lax.axis_index("sp")
    mine = find(owner_ref, me)
    prompt = mine // MAX_STRETCHES
    own = mine % MAX_STRETCHES
    length = length_ref[prompt]
    lanes = q_ref.shape[0]
    group, block, turn = pl.program_id(0), pl.program_id(1), pl.program_id(2)
    columns = pl.ds(pl.multiple_of(group * HEAD_DIM, HEAD_DIM), HEAD_DIM)
    copies = [
        pltpu.make_async_copy(stage.at[i], out.at[:, columns], sems.at[i])
        for i, out in enumerate((kc_ref, vc_ref))
    ]

    @pl.when((block == 0) & (turn == 0))
    def _():
        homed = jnp.int32(0)
        kept = jnp.int32(0)
        for p in range(home_ref.shape[0]):
            here = home_ref[p] == me
            homed = jnp.where(here, p, homed)
            kept = jnp.where(here, length_ref[p], kept)

        def fill(j, _):
            start = pl.multiple_of(owner_ref[homed * MAX_STRETCHES + j] * stretch, stretch)
            target = pl.ds(pl.multiple_of(j * stretch, stretch), stretch)
            position = j * stretch + lax.broadcasted_iota(jnp.int32, (stretch, HEAD_DIM), 0)
            for i, source in enumerate((k_ref, v_ref)):
                block = source[pl.ds(start, stretch), :]
                stage[i, target, :] = jnp.where(position < kept, block, jnp.zeros_like(block))
            return 0

        lax.fori_loop(0, MAX_STRETCHES, fill, 0)
        for copy in copies:
            copy.start()

        def turned(j, _):
            rows = pl.ds(pl.multiple_of(j * stretch, stretch), stretch)
            vt_ref[:HEAD_DIM, rows] = v_ref[rows, :].T
            return 0

        lax.fori_loop(0, v_ref.shape[0] // stretch, turned, 0)
        vt_ref[HEAD_DIM:, :] = jnp.ones((16, v_ref.shape[0]), jnp.bfloat16)

    within = block * lanes + lax.broadcasted_iota(jnp.int32, (1, lanes), 1)
    live = own * stretch + block * lanes < length

    @pl.when(live)
    def _():
        scale = HEAD_DIM ** (-0.5) * LOG2E
        piece = stretch // 2

        def first_row(j):
            return pl.multiple_of(owner_ref[prompt * MAX_STRETCHES + j] * stretch, stretch)

        def score(j, u, c):
            rows = pl.ds(first_row(j) + c * piece, piece)
            query = q_ref[:, u * HEAD_DIM : (u + 1) * HEAD_DIM]
            scores = lax.dot_general(
                k_ref[rows, :], query, (((1,), (1,)), ((), ())), preferred_element_type=jnp.float32
            )
            score_ref[u, c * piece : (c + 1) * piece, :] = scores
            return jnp.max(scores, axis=0, keepdims=True)

        def score_all(j, u):
            highest = [score(j, u, c) for c in range(2)]
            high_ref[u] = functools.reduce(jnp.maximum, highest)

        def spread(j, u, masked, ahead):
            top = top_ref[u]
            start = first_row(j)
            if masked:
                def seen(c):
                    place_of = c * piece + lax.broadcasted_iota(jnp.int32, (piece, lanes), 0)
                    part = score_ref[u, c * piece : (c + 1) * piece, :]
                    return jnp.where(place_of <= within, part, FAR)

                high = functools.reduce(
                    jnp.maximum,
                    [jnp.max(seen(c), axis=0, keepdims=True) for c in range(2)],
                )
            else:
                def seen(c):
                    return score_ref[u, c * piece : (c + 1) * piece, :]

                high = high_ref[u]
            new_top = jnp.maximum(top, high * scale)
            rescale = jnp.exp2(top - new_top)
            highest, weights = [], []
            acc = acc_ref[u] * rescale
            for c in range(2):
                if ahead is not None:
                    highest.append(score(ahead[0], ahead[1], c))
                weights.append(jnp.exp2(seen(c) * scale - new_top).astype(jnp.bfloat16))
            acc = acc + jnp.dot(
                vt_ref[:, pl.ds(start, stretch)], jnp.concatenate(weights, axis=0),
                preferred_element_type=jnp.float32,
            )
            acc_ref[u] = acc
            top_ref[u] = new_top
            if ahead is not None:
                high_ref[ahead[1]] = functools.reduce(jnp.maximum, highest)

        top_ref[...] = jnp.full_like(top_ref, FAR)
        acc_ref[...] = jnp.zeros_like(acc_ref)
        score_all(0, 0)

        def body(j, _):
            for u in range(heads):
                spread(j, u, False, (j, u + 1) if u + 1 < heads else (j + 1, 0))
            return 0

        lax.fori_loop(0, own, body, 0)
        for u in range(heads):
            spread(own, u, True, (own, u + 1) if u + 1 < heads else None)
        alive = (own * stretch + within < length).astype(jnp.float32)
        for u in range(heads):
            out = (acc_ref[u, :HEAD_DIM] * (alive / acc_ref[u, HEAD_DIM : HEAD_DIM + 1])).T
            o_ref[:, u * HEAD_DIM : (u + 1) * HEAD_DIM] = out.astype(jnp.bfloat16)

    @pl.when(jnp.logical_not(live))
    def _():
        o_ref[...] = jnp.zeros_like(o_ref)

    @pl.when((block == pl.num_programs(1) - 1) & (turn == pl.num_programs(2) - 1))
    def _():
        for copy in copies:
            copy.wait()


def attend(stretch, tables, queries, keys, values):
    width = queries.shape[1]
    kv_width = keys.shape[1]
    local_kv = kv_width // HEAD_DIM
    group_size = width // kv_width
    heads = math.gcd(UNROLL, group_size)
    turns = group_size // heads
    lanes = math.gcd(ROW_BLOCK, stretch)
    span = MAX_STRETCHES * stretch
    cache = jax.ShapeDtypeStruct((span, kv_width), jnp.bfloat16)
    query_spec = pl.BlockSpec((lanes, heads * HEAD_DIM), lambda g, r, u, *_: (r, g * turns + u))
    kv_spec = pl.BlockSpec((keys.shape[0], HEAD_DIM), lambda g, r, u, *_: (0, g))
    return pl.pallas_call(
        functools.partial(attend_kernel, stretch, heads),
        out_shape=[jax.ShapeDtypeStruct((stretch, width), jnp.bfloat16), cache, cache],
        grid_spec=pltpu.PrefetchScalarGridSpec(
            num_scalar_prefetch=3,
            grid=(local_kv, stretch // lanes, turns),
            in_specs=[query_spec, kv_spec, kv_spec],
            out_specs=[query_spec] + [pl.BlockSpec(memory_space=pl.ANY)] * 2,
            scratch_shapes=[
                pltpu.VMEM((2, span, HEAD_DIM), jnp.bfloat16),
                pltpu.SemaphoreType.DMA((2,)),
                pltpu.VMEM((heads, 1, lanes), jnp.float32),
                pltpu.VMEM((heads, 1, lanes), jnp.float32),
                pltpu.VMEM((heads, HEAD_DIM + 16, lanes), jnp.float32),
                pltpu.VMEM((HEAD_DIM + 16, values.shape[0]), jnp.bfloat16),
                pltpu.VMEM((heads, stretch, lanes), jnp.float32),
            ],
        ),
        compiler_params=pltpu.CompilerParams(
            dimension_semantics=("arbitrary",) * 3, vmem_limit_bytes=48 * 2**20
        ),
        name="attend",
    )(*tables, queries, keys, values)


def gather_kernel(k_ref, v_ref, all_k, all_v, place_sem, send_sem, recv_sem):
    me = lax.axis_index("sp")
    rows = k_ref.shape[0]
    y, x, core = me // 4, me // 2 % 2, me % 2
    index = lambda y, x, core: y * 4 + x * 2 + core
    beside = index(y, 1 - x, core)
    above = index(1 - y, x, core)
    across = index(1 - y, 1 - x, core)
    partner = index(y, x, 1 - core)
    relay_from = core * beside + (1 - core) * above
    relay_to = core * above + (1 - core) * beside
    half = rows // 2
    count = 4
    sources = [ref.at[pl.ds(h * half, half), :] for ref in (k_ref, v_ref) for h in range(2)]
    outs = [(ref, h) for ref in (all_k, all_v) for h in range(2)]

    barrier = pltpu.get_barrier_semaphore()
    for other in (beside, above, partner):
        pl.semaphore_signal(barrier, inc=1, device_id={"sp": other}, device_id_type=MESH)
    pl.semaphore_wait(barrier, 3)

    def part(place, owner):
        ref, h = place
        return ref.at[pl.ds(pl.multiple_of(owner * rows + h * half, half), half), :]

    def send(i, lane, source, owner, target):
        return pltpu.make_async_remote_copy(
            src_ref=source,
            dst_ref=part(outs[i], owner),
            send_sem=send_sem.at[lane, i],
            recv_sem=recv_sem.at[lane, i],
            device_id={"sp": target},
            device_id_type=MESH,
        )

    sent = []
    for i in range(count):
        for lane, target in ((0, beside), (1, above), (2, partner)):
            copy = send(i, lane, sources[i], me, target)
            copy.start()
            sent.append(copy)
        own = pltpu.make_async_copy(sources[i], part(outs[i], me), place_sem.at[i])
        own.start()
    relays = []
    for i in range(count):
        sent[3 * i].wait_recv()
        sent[3 * i + 1].wait_recv()
        relay = send(i, 3, part(outs[i], relay_from), relay_from, relay_to)
        relay.start()
        relays.append(relay)
        for lane, owner in ((4, beside), (5, above)):
            copy = send(i, lane, part(outs[i], owner), owner, partner)
            copy.start()
            relays.append(copy)
    last = []
    for i in range(count):
        relays[3 * i].wait_recv()
        copy = send(i, 6, part(outs[i], across), across, partner)
        copy.start()
        last.append(copy)
    for i in range(count):
        sent[3 * i + 2].wait_recv()
        relays[3 * i + 1].wait_recv()
        relays[3 * i + 2].wait_recv()
        last[i].wait_recv()
        pltpu.make_async_copy(sources[i], part(outs[i], me), place_sem.at[i]).wait()
    for copy in sent + relays + last:
        copy.wait_send()


def gather(keys, values):
    replicas = lax.axis_size("sp")
    if replicas != 8:
        return (
            lax.all_gather(keys, "sp", axis=0, tiled=True),
            lax.all_gather(values, "sp", axis=0, tiled=True),
        )
    shape = jax.ShapeDtypeStruct((replicas * keys.shape[0], keys.shape[1]), keys.dtype)
    return pl.pallas_call(
        gather_kernel,
        out_shape=[shape] * 2,
        in_specs=[pl.BlockSpec(memory_space=pltpu.VMEM)] * 2,
        out_specs=[pl.BlockSpec(memory_space=pl.ANY)] * 2,
        scratch_shapes=[
            pltpu.SemaphoreType.DMA((4,)),
            pltpu.SemaphoreType.DMA((7, 4)),
            pltpu.SemaphoreType.DMA((7, 4)),
        ],
        compiler_params=pltpu.CompilerParams(collective_id=0, has_side_effects=True),
        name="gather",
    )(keys, values)


def project_kernel(
    steps, a_ref, w_ref, o_ref, work, own, out_far, out_near, out_sum,
    in_far, in_near, in_sum, send_sem, recv_sem,
):
    me = lax.axis_index("tp")
    n = 4
    rows = a_ref.shape[0] // n
    step = pl.program_id(0)

    def hops(j):
        turn = 1 - 2 * (j % 2)
        return (me + turn + n) % n, (me - turn + n) % n

    def send(kind, j, target):
        source, dest = ((out_far, in_far), (out_near, in_near), (out_sum, in_sum))[kind]
        return pltpu.make_async_remote_copy(
            src_ref=source.at[j],
            dst_ref=dest.at[j],
            send_sem=send_sem.at[kind, j],
            recv_sem=recv_sem.at[kind, j],
            device_id={"tp": target},
            device_id_type=MESH,
        )

    @pl.when(step == 0)
    def _():
        barrier = pltpu.get_barrier_semaphore()
        for other in ((me + 1) % n, (me + n - 1) % n):
            pl.semaphore_signal(barrier, inc=1, device_id={"tp": other}, device_id_type=MESH)
        pl.semaphore_wait(barrier, 2)

    def rows_of(device):
        return pl.ds(pl.multiple_of(device * rows, rows), rows)

    def relay(j):
        toward, away = hops(j)
        send(0, j, toward).wait_recv()
        total = work[j % 2, rows_of(toward), :] + in_far[j].astype(jnp.float32)
        out_sum[j] = total.astype(jnp.bfloat16)
        send(2, j, toward).start()

    toward, away = hops(step)
    work[step % 2] = jnp.dot(a_ref[...], w_ref[...], preferred_element_type=jnp.float32)
    out_far[step] = work[step % 2, rows_of((me + 2) % n), :].astype(jnp.bfloat16)
    send(0, step, toward).start()
    out_near[step] = work[step % 2, rows_of(away), :].astype(jnp.bfloat16)
    send(1, step, away).start()
    own[step] = work[step % 2, rows_of(me), :]

    @pl.when(step > 0)
    def _():
        relay(step - 1)

    @pl.when(step == steps - 1)
    def _():
        relay(step)
        width = o_ref.shape[1] // steps
        for j in range(steps):
            toward, away = hops(j)
            send(1, j, away).wait_recv()
            send(2, j, toward).wait_recv()
            total = own[j] + in_near[j].astype(jnp.float32) + in_sum[j].astype(jnp.float32)
            o_ref[:, j * width : (j + 1) * width] = total.astype(jnp.bfloat16)
        for j in range(steps):
            toward, away = hops(j)
            send(0, j, toward).wait_send()
            send(1, j, away).wait_send()
            send(2, j, toward).wait_send()


def project(attended, w_out):
    if lax.axis_size("tp") != 4:
        partial = jnp.dot(attended, w_out, preferred_element_type=jnp.float32)
        return lax.psum_scatter(
            partial.astype(jnp.bfloat16), "tp", scatter_dimension=0, tiled=True
        )
    tokens, depth = attended.shape
    features = w_out.shape[1]
    rows = tokens // 4
    steps = 8
    width = features // steps
    buffer = pltpu.VMEM((steps, rows, width), jnp.bfloat16)
    return pl.pallas_call(
        functools.partial(project_kernel, steps),
        out_shape=jax.ShapeDtypeStruct((rows, features), jnp.bfloat16),
        grid=(steps,),
        in_specs=[
            pl.BlockSpec((tokens, depth), lambda j: (0, 0)),
            pl.BlockSpec((depth, width), lambda j: (0, j)),
        ],
        out_specs=pl.BlockSpec((rows, features), lambda j: (0, 0)),
        scratch_shapes=[
            pltpu.VMEM((2, tokens, width), jnp.float32),
            pltpu.VMEM((steps, rows, width), jnp.float32),
            buffer, buffer, buffer, buffer, buffer, buffer,
            pltpu.SemaphoreType.DMA((3, steps)),
            pltpu.SemaphoreType.DMA((3, steps)),
        ],
        compiler_params=pltpu.CompilerParams(
            collective_id=1,
            has_side_effects=True,
            dimension_semantics=("arbitrary",),
            vmem_limit_bytes=48 * 2**20,
        ),
        name="project",
    )(attended, w_out)


def shards(queries, keys, values, w_out, lengths, stretch_owner, home_replica):
    stretch = queries.shape[0]
    tables = (stretch_owner, lengths, home_replica)
    all_keys, all_values = gather(keys, values)
    attended, kept_keys, kept_values = attend(stretch, tables, queries, all_keys, all_values)
    return (project(attended, w_out), kept_keys, kept_values)


def solution(mesh):
    placed = (P("sp", "tp"), P("sp", "tp"), P("sp", "tp"), P("tp", None), P(), P(), P())
    return jax.shard_map(
        shards,
        mesh=mesh,
        in_specs=placed,
        out_specs=(P(("sp", "tp"), None), P("sp", "tp"), P("sp", "tp")),
        check_vma=False,
    )
```
